32 devices in a mesh: row: 4 (over y, x), col: 8 (over z, core).
Axes of the slice: x: 2, y: 2, z: 4, core: 2. Of those that a mesh axis runs over, the one named last changes fastest.
Arguments:
- u_field: float32 [128, 8192], P('row', 'col'), may hold values from -4 to 4
- v_field: float32 [128, 8192], P('row', 'col'), may hold values from -7.5 to 7.5
- stimulus: float32 [128, 8192], P('row', 'col'), may hold values from -6 to 6
Outputs:
- u_final: float32 [128, 8192], P('row', 'col')
- v_final: float32 [128, 8192], P('row', 'col')
The draws below stay inside these ranges and needn't reach their ends.
All inputs are finite; a program needn't handle non-finite values.
Results may differ from the reference program's by a relative error of at most 0.0003.
Values sent between devices are 32-bit elements; how exact they have to be, the bound alone decides.
No kernel may reach another device: no remote copies, remote signals or barrier semaphores. Data moves between devices by JAX's collectives and lax.ppermute only.
A program may use at most 64 MiB of HBM per device.

```python
import jax
import jax.numpy as jnp
from jax import lax

MICRO_COUNT = 4
MIDDLE = 3
TOP = 3
OUTER = 2
NROWS = 128
NCOLS = 8192


def draw_v_field(key, part):
    first_key, second_key, third_key = jax.random.split(key, 3)
    row_stripes = (NROWS + 7) // 8
    col_stripes = (NCOLS + 7) // 8
    row_levels = jax.random.uniform(first_key, (row_stripes,), minval=-3.0, maxval=3.0)
    col_levels = jax.random.uniform(second_key, (col_stripes,), minval=-3.0, maxval=3.0)
    roughness = 0.5 * jax.random.truncated_normal(third_key, -3.0, 3.0, (NROWS, NCOLS))
    row_index = jnp.arange(NROWS) // 8
    col_index = jnp.arange(NCOLS) // 8
    combined = row_levels[row_index][:, None] + col_levels[col_index][None, :] + roughness
    return combined.astype(jnp.float32)


def levels(rng, shape, cuts, least, largest):
    loudness = 1.0
    for position, shards_of in cuts:
        draws = jax.random.uniform(jax.random.fold_in(jax.random.fold_in(rng, 6), position), (shards_of,), jnp.float32, least / len(cuts), largest / len(cuts))
        loudness = loudness * jnp.repeat(jnp.exp(draws), shape[position] // shards_of).reshape((-1,) + (1,) * (len(shape) - 1 - position))
    return loudness


def centred(own_key, dims, scale, reach, shards=(), kind=jnp.bfloat16):
    entries = scale * jax.random.normal(own_key, dims, jnp.float32)
    if shards:
        entries = entries * levels(own_key, dims, shards, -0.22, 0.18)
    return jnp.clip(entries, -reach, reach).astype(kind)


def setup_inputs(seed: int = 0) -> dict:
    seeds = jax.random.split(jax.random.key(seed), 4)
    return {
        "u_field": centred(seeds[0], (NROWS, NCOLS), 1.0, 4.0, ((0, 4), (1, 8)), jnp.float32),
        "v_field": draw_v_field(jax.random.fold_in(seeds[3], 71), 0),
        "stimulus": centred(seeds[2], (NROWS, NCOLS), 0.5, 6.0, ((0, 4), (1, 8)), jnp.float32),
    }


RATE_U = 0.125
RATE_V = 0.125
TIME_STEP = 0.05
RECOVERY = 0.08
OFFSET = 0.7
DAMPING = 0.8


def neighbours(grid):
    total = jnp.roll(grid, 1, 0) + jnp.roll(grid, -1, 0)
    total = total + jnp.roll(grid, 1, 1) + jnp.roll(grid, -1, 1)
    return total - 4.0 * grid


def advance(fields, stimulus):
    u_now, v_now = fields
    u_next = u_now + RATE_U * neighbours(u_now) + TIME_STEP * (u_now - u_now * u_now * u_now / 3.0 - v_now + stimulus)
    v_next = v_now + RATE_V * neighbours(v_now) + TIME_STEP * RECOVERY * (u_now + OFFSET - DAMPING * v_now)
    return (u_next, v_next)


def forward_linear_jump(inner, repeats):
    def run(fields):
        def turn(present_index, pair_now):
            return (pair_now[1], inner(pair_now[1]))
        previous_fields, latest = lax.fori_loop(0, repeats, turn, (fields, fields))
        return jax.tree.map(lambda last, prior: last + (last - prior), latest, previous_fields)
    return run


def reference(u_field, v_field, stimulus):
    def euler_micro_update(fields):
        return advance(fields, stimulus)
    coarse_state_vector = forward_linear_jump(euler_micro_update, MICRO_COUNT)
    second = forward_linear_jump(coarse_state_vector, MIDDLE)
    third = forward_linear_jump(second, TOP)
    final_fields = lax.fori_loop(0, OUTER, lambda present_index, fields: third(fields), (u_field, v_field))
    return final_fields[0], final_fields[1]
```

```python
import functools

import jax
import jax.numpy as jnp
from jax import lax
from jax.experimental import pallas as pl
from jax.experimental.pallas import tpu as pltpu
from jax.sharding import PartitionSpec as P

MICRO_COUNT = 4
MIDDLE = 3
TOP = 3
OUTER = 2

RATE = 0.125
TIME_STEP = 0.05
RECOVERY = 0.08
OFFSET = 0.7
DAMPING = 0.8

CENTRE = OFFSET / DAMPING
UNIT_U = (3.0 * RATE / TIME_STEP) ** 0.5
UNIT_V = UNIT_U * RATE / TIME_STEP
KEEP_U = (1.0 - 4.0 * RATE + TIME_STEP) / RATE
KEEP_V = (1.0 - 4.0 * RATE - TIME_STEP * RECOVERY * DAMPING) / RATE
FEED = TIME_STEP * RECOVERY * UNIT_U / (UNIT_V * RATE)

P1 = MICRO_COUNT
P2 = P1 * MIDDLE
P3 = P2 * TOP
STEPS = P3 * OUTER
RING = MIDDLE + 1
SUB = 8
LANE = 128


def up(value, unit):
    return -(-value // unit) * unit


class Layout:
    def __init__(self, rows, cols, height, width):
        self.rows, self.cols = rows, cols
        self.height, self.width = height, width
        self.lanes = rows * height
        self.chunk = width // rows
        self.half = self.chunk // 2
        self.reach = up(STEPS, SUB)
        self.paired = rows & (rows - 1) == 0
        assert width % rows == 0 and self.chunk % LANE == 0
        assert height % SUB == 0 and self.chunk >= self.reach
        self.rank = [self._rank(i) for i in range(rows)]

    def _rank(self, i):
        if not self.paired:
            return i
        rank = 0
        while i:
            rank ^= i
            i >>= 1
        return rank

    def place(self, i, c):
        if isinstance(i, int):
            rank = self.rank[i]
        else:
            rank = sum(jnp.where(i == k, r, 0) for k, r in enumerate(self.rank))
        return rank + (c % 2) * (self.rows - 1 - 2 * rank)

    def target(self, i, d):
        return i ^ d if self.paired else (i + d) % self.rows

    def source(self, i, d):
        return i ^ d if self.paired else (i + self.rows - d) % self.rows

    def to_rows(self, d):
        return [(i, self.target(i, d)) for i in range(self.rows)]

    def ring(self, shift):
        line = {}
        for c in range(self.cols):
            for i in range(self.rows):
                line[c * self.rows + self.place(i, c)] = i * self.cols + c
        count = len(line)
        return [(line[q], line[(q + shift) % count]) for q in range(count)]

    def inner(self, t):
        return range(0, max(0, -(-(self.half - t) // SUB)))

    def low(self, t):
        return max(0, (self.half - t) // SUB)

    def outer(self, t):
        return range(self.low(t), -(-(self.half + self.reach - t) // SUB))

    def handed(self):
        have = {0: self.low(0)}
        need = []

        def want(time, block):
            for b in range(block, have[time]):
                need.append((time, b))
            have[time] = min(have[time], block)

        for t in range(1, STEPS + 1):
            low = self.low(t)
            want(t - 1, low)
            if t % P2 == 0:
                want(t - P1, low)
            if t % P3 == 0:
                want(t - P2, low)
            have[t] = low
        return sorted(need)


def even_lane(shape):
    return lax.broadcasted_iota(jnp.int32, shape, 1) % 2 == 0


def here():
    return lax.axis_index("row"), lax.axis_index("col")


def columns(lay, i, c):
    return pl.ds(pl.multiple_of(lay.place(i, c) * lay.chunk, LANE), lay.chunk)


def rows_of(lay, i):
    return pl.ds(pl.multiple_of(i * lay.height, SUB), lay.height)


def reverse_lanes(x):
    index = LANE - 1 - lax.broadcasted_iota(jnp.int32, x.shape, 1)
    return jnp.take_along_axis(x, index, axis=1)


def pack_kernel(lay, u, v, s, *refs):
    outs, ready = refs[: lay.rows], refs[lay.rows]
    i, c = here()
    copies = []
    for d in range(lay.rows):
        for f, field in enumerate((u, v, s)):
            part = field.at[:, columns(lay, lay.target(i, d), c)]
            copies.append(pltpu.make_async_copy(part, outs[d].at[f], ready.at[3 * d + f]))
    for copy in copies:
        copy.start()
    for copy in copies:
        copy.wait()


def interleave(lay, left, right):
    even = even_lane(left.shape)
    n = lay.lanes
    return (
        jnp.where(even, left, pltpu.roll(right, 1, 1)),
        jnp.where(even, pltpu.roll(left, n - 1, 1), right),
    )


def turn_kernel(lay, *refs):
    moved = refs[: lay.rows]
    state, drive, first, last, board = refs[lay.rows :]
    i, _ = here()
    tiles = lay.chunk // LANE
    for f in range(3):
        for d in range(lay.rows):
            board[f, rows_of(lay, lay.source(i, d)), :] = moved[d][f]
    for f in range(3):
        shift, scale = ((0.0, 1.0 / UNIT_U), (CENTRE, 1.0 / UNIT_V), (CENTRE, 1.0 / UNIT_V))[f]
        parts = [(board[f, :, a * LANE : (a + 1) * LANE] - shift) * scale for a in range(tiles)]
        ahead = jnp.concatenate([x.T for x in parts], axis=0)
        back = jnp.concatenate([reverse_lanes(x).T for x in reversed(parts)], axis=0)
        first[f] = ahead[: lay.reach]
        last[f] = back[: lay.reach]
        zero, one = interleave(lay, back[lay.half :], ahead[lay.half :])
        if f < 2:
            state[2 * f] = zero
            state[2 * f + 1] = one
        else:
            drive[0] = zero
            drive[1] = one


class Stage:
    def __init__(self, lay, kept, micro, offset, drive):
        self.lay, self.kept, self.micro, self.offset, self.drive = lay, kept, micro, offset, drive

    def at(self, t):
        if t % P1:
            return self.micro.at[t % P1 - 1]
        return self.kept.at[t // P1 % RING]

    def block(self, b):
        return pl.ds(self.offset + SUB * b, SUB)

    def line(self, x):
        return pl.ds(self.offset + x, 1)

    def fold(self, t, part, y):
        n = self.lay.lanes
        swapped = jnp.where(even_lane(y.shape), pltpu.roll(y, n - 1, 1), pltpu.roll(y, 1, 1))
        self.at(t)[part, self.line(-1), :] = swapped[0:1]

    def step(self, t, blocks):
        n = self.lay.lanes
        src, dst = self.at(t - 1), self.at(t)
        jump = t % P1 == 0
        second = t % P2 == 0
        third = t % P3 == 0
        scale = RATE * (2 if jump else 1) * (2 if second else 1) * (2 if third else 1)
        less = 0.5 / RATE if jump else 0.0
        for b in blocks:
            r = self.offset + SUB * b
            centre = [src[p, pl.ds(r, SUB), :] for p in range(4)]
            beside = [src[p, pl.ds(r - 1, SUB), :] + src[p, pl.ds(r + 1, SUB), :] for p in range(4)]
            for k in range(2):
                u, v = centre[k], centre[2 + k]
                other_u, other_v = centre[1 - k], centre[3 - k]
                turn = (2, n - 2)[k]
                near_u = beside[k] + (other_u + pltpu.roll(other_u, turn, 1))
                near_v = beside[2 + k] + (other_v + pltpu.roll(other_v, turn, 1))
                next_u = near_u + u * (KEEP_U - less - u * u) + (self.drive(k, b) - v)
                next_v = near_v + (v * (KEEP_V - less) + u * FEED)
                for part, y in ((k, next_u), (2 + k, next_v)):
                    if scale != 1.0:
                        y = y * scale
                    if second:
                        old = self.at(t - P1)[part, pl.ds(r, SUB), :]
                        if third:
                            old = old + old + self.at(t - P2)[part, pl.ds(r, SUB), :]
                        y = y - old
                    dst[part, pl.ds(r, SUB), :] = y
                    if b == 0:
                        self.fold(t, part, y)


def inner_kernel(lay, state, drive, lines, blocks, done, kept, micro):
    stage = Stage(lay, kept, micro, SUB, lambda k, b: drive[k, pl.ds(SUB * b, SUB), :])
    handed = lay.handed()
    for part in range(4):
        kept[0, part, SUB : SUB + lay.half, :] = state[part]
        stage.fold(0, part, state[part, 0:SUB, :])
    for t in range(STEPS + 1):
        if t:
            stage.step(t, lay.inner(t))
        if t == STEPS:
            break
        now = stage.at(t)
        low = lay.low(t + 1)
        for part in range(4):
            if low:
                lines[part, t : t + 1, :] = now[part, stage.line(SUB * low - 1), :]
            for j, (time, b) in enumerate(handed):
                if time == t:
                    blocks[part, SUB * j : SUB * j + SUB, :] = now[part, stage.block(b), :]
    final = lay.low(STEPS) * SUB
    if final:
        for part in range(4):
            done[part, 0:final, :] = stage.at(STEPS)[part, SUB : SUB + final, :]


def outer_kernel(lay, drive, lines, blocks, done, left, right, *refs):
    outs, (kept, micro, halo, board) = refs[: lay.rows], refs[lay.rows :]
    i, c = here()
    half, n = lay.half, lay.lanes

    def push(k, b):
        if SUB * b < half:
            return drive[k, pl.ds(SUB * b, SUB), :]
        return halo[k, pl.ds(SUB * b - half, SUB), :]

    base = SUB * lay.low(STEPS) - SUB
    stage = Stage(lay, kept, micro, -base, push)
    handed = lay.handed()
    for f in range(3):
        pair = interleave(lay, left[f], right[f])
        for k in range(2):
            if f < 2:
                kept[0, 2 * f + k, half - base : half - base + lay.reach, :] = pair[k]
            else:
                halo[k] = pair[k]
    for t in range(STEPS + 1):
        if t:
            stage.step(t, lay.outer(t))
        if t == STEPS:
            break
        now = stage.at(t)
        low = lay.low(t + 1)
        for part in range(4):
            if low:
                now[part, stage.line(SUB * low - 1), :] = lines[part, t : t + 1, :]
            for j, (time, b) in enumerate(handed):
                if time == t:
                    now[part, stage.block(b), :] = blocks[part, SUB * j : SUB * j + SUB, :]
                    if b == 0:
                        stage.fold(t, part, blocks[part, SUB * j : SUB * j + SUB, :])
    final = lay.low(STEPS) * SUB
    tiles = lay.chunk // LANE
    for f in range(2):
        pair = []
        for k in range(2):
            y = stage.at(STEPS)[2 * f + k, final - base : half - base, :]
            if final:
                y = jnp.concatenate([done[2 * f + k, 0:final, :], y], axis=0)
            pair.append(y * UNIT_V + CENTRE if f else y * UNIT_U)
        even = even_lane(pair[0].shape)
        west = jnp.where(even, pair[0], pltpu.roll(pair[1], 1, 1))
        east = jnp.where(even, pltpu.roll(pair[0], n - 1, 1), pair[1])
        if half % LANE:
            west, east = (jnp.concatenate([z[: LANE - half % LANE], z], axis=0) for z in (west, east))
        for a in range(tiles):
            lo, hi = a * LANE, (a + 1) * LANE
            skip = lay.chunk - east.shape[0]
            natural = reverse = None
            if hi > half:
                natural = east[lo - skip : hi - skip].T
            if lo < half:
                back = (tiles - 1 - a) * LANE - skip
                reverse = reverse_lanes(west[back : back + LANE].T)
            if natural is None:
                tile = reverse
            elif reverse is None:
                tile = natural
            else:
                lane = lax.broadcasted_iota(jnp.int32, natural.shape, 1)
                tile = jnp.where(lane < half - lo, reverse, natural)
            board[f, :, lo:hi] = tile
        for d in range(lay.rows):
            outs[d][f] = board[f, rows_of(lay, lay.target(i, d)), :]


def place_kernel(lay, *refs):
    pieces, (u, v) = refs[: lay.rows], refs[lay.rows :]
    i, c = here()
    for d in range(lay.rows):
        for f, out in enumerate((u, v)):
            out[:, columns(lay, lay.source(i, d), c)] = pieces[d][f]


def shape(*dims):
    return jax.ShapeDtypeStruct(dims, jnp.float32)


def call(kernel, lay, outs, scratch, name, mib, **specs):
    return pl.pallas_call(
        functools.partial(kernel, lay),
        out_shape=outs,
        **specs,
        scratch_shapes=[pltpu.VMEM(x, jnp.float32) if isinstance(x, tuple) else x for x in scratch],
        compiler_params=pltpu.CompilerParams(vmem_limit_bytes=mib * 2**20),
        name=name,
    )


def body(lay, u_field, v_field, stimulus):
    r, h, w, n = lay.rows, lay.height, lay.chunk, lay.lanes
    half, reach = lay.half, lay.reach
    fields = (u_field, v_field, stimulus)
    packs = call(
        pack_kernel,
        lay,
        [shape(3, h, w)] * r,
        [pltpu.SemaphoreType.DMA((3 * r,))],
        "pack",
        8,
        in_specs=[pl.BlockSpec(memory_space=pltpu.HBM)] * 3,
    )(*fields)
    moved = [packs[0]] + [lax.ppermute(packs[d], "row", lay.to_rows(d)) for d in range(1, r)]
    state, drive, first, last = call(
        turn_kernel,
        lay,
        [shape(4, half, n), shape(2, half, n), shape(3, reach, n), shape(3, reach, n)],
        [(3, n, w)],
        "turn",
        8,
    )(*moved)
    right = lax.ppermute(first, ("row", "col"), lay.ring(-1))
    left = lax.ppermute(last, ("row", "col"), lay.ring(1))
    extra = max(1, len(lay.handed()))
    final = max(1, lay.low(STEPS))
    lines, blocks, done = call(
        inner_kernel,
        lay,
        [shape(4, reach, n), shape(4, SUB * extra, n), shape(4, SUB * final, n)],
        [(RING, 4, half + 2 * SUB, n), (P1 - 1, 4, half + 2 * SUB, n)],
        "inner",
        16,
    )(state, drive)
    span = half + reach + 2 * SUB - SUB * lay.low(STEPS)
    pieces = call(
        outer_kernel,
        lay,
        [shape(2, h, w)] * r,
        [(RING, 4, span, n), (P1 - 1, 4, span, n), (2, reach, n), (2, n, w)],
        "outer",
        24,
    )(drive, lines, blocks, done, left, right)
    back = [pieces[0]] + [lax.ppermute(pieces[d], "row", lay.to_rows(d)) for d in range(1, r)]
    return tuple(
        call(place_kernel, lay, [shape(h, lay.width)] * 2, [], "place", 8)(*back)
    )


def solution(mesh):
    def run(u_field, v_field, stimulus):
        lay = Layout(mesh.shape["row"], mesh.shape["col"], *u_field.shape)
        return body(lay, u_field, v_field, stimulus)

    return jax.shard_map(
        run,
        mesh=mesh,
        in_specs=(P("row", "col"),) * 3,
        out_specs=(P("row", "col"),) * 2,
        check_vma=False,
    )
```
